32 devices in a mesh: island: 4 (over y, x), shard: 8 (over z, core).
Axes of the slice: x: 2, y: 2, z: 4, core: 2. Of those that a mesh axis runs over, the one named last changes fastest.
Arguments:
- gate_pre: bfloat16 [16384, 256], P(('island', 'shard')), may hold values from -6 to 6
- up_pre: bfloat16 [16384, 256], P(('island', 'shard')), may hold values from -6 to 6
- grad_out: bfloat16 [16384, 8192], P(('island', 'shard')), may hold values from -6 to 6
- token_ids: int32 [16384], P(('island', 'shard')), may hold values from 0 to 128255, as said below
- step_count: int32 [1], replicated, may hold values from 0 to 999
- island_drift: float32 [4, 256, 8192], P('island', 'shard'), may hold values from -4 to 4
- adam_m: float32 [4, 256, 8192], P('island', 'shard'), may hold values from -0.015625 to 0.015625
- adam_v: float32 [4, 256, 8192], P('island', 'shard'), may hold values from 3.8146972e-08 to 6.1035155e-07
- anchor: float32 [256, 8192], P('shard'), may hold values from -6 to 6
- momentum: float32 [256, 8192], P('shard'), may hold values from -4 to 4
- next_hidden: bfloat16 [16384, 256], P(('island', 'shard')), may hold values from -6 to 6
Outputs:
- new_anchor: float32 [256, 8192], P('shard', 'island')
- new_momentum: float32 [256, 8192], P('shard', 'island')
- next_out: bfloat16 [16384, 8192], P(('island', 'shard'))
- live_share: float32 [4], P('island')
The draws below stay inside these ranges and needn't reach their ends.
Inputs may be any that keep to these rules, and one draw needn't show every extreme that they name: `token_ids`: 0 marks padding; within each aligned block of 512 rows the padding comes last, and a third or more of the block's rows are tokens.
All inputs are finite; a program needn't handle non-finite values.
Results may differ from the reference program's by a relative error of at most 0.0004.
The reference program's roundings to bfloat16 on the way (of `hidden`, `masked` and `weights`) count: a program that leaves them out, or rounds other values in their place, can miss the bound.
Values may be sent and summed in bfloat16 or wider, within the bound.
A program may use at most 128 MiB of HBM per device.

```python
import math
import jax
import jax.numpy as jnp
from jax import lax

D = 8192
VOCAB = 128256
TOK_DEV = 512
FF = 256
TOK_ISLAND = 4096
TOKENS = 16384
N_ISLAND = 4
N_SHARD = 8


def draw_token_ids(key, part):
    total_rows = TOK_DEV * N_ISLAND * N_SHARD
    blocks = N_ISLAND * N_SHARD
    key_ids, key_cut = jax.random.split(jax.random.fold_in(key, 17))
    fresh_ids = jax.random.randint(key_ids, (total_rows,), 1, VOCAB)
    jitter = jax.random.randint(key_cut, (blocks,), 0, max(TOK_DEV // 16, 1))
    shard_rank = jnp.arange(blocks, dtype=jnp.int32) % N_SHARD
    lower_half = (shard_rank < N_SHARD // 2).astype(jnp.int32)
    cut_rows = lower_half * (3 * TOK_DEV // 5 + jitter)
    live_count = TOK_DEV - cut_rows
    within_block = jnp.arange(total_rows, dtype=jnp.int32) % TOK_DEV
    live_rows = jnp.repeat(live_count, TOK_DEV)
    return jnp.where(within_block < live_rows, fresh_ids, 0).astype(jnp.int32)


def shard_levels(own_key, shape, cuts, smallest, top_value):
    gain = 1.0
    for axis_at, parts in cuts:
        heights = jax.random.uniform(jax.random.fold_in(jax.random.fold_in(own_key, 6), axis_at), (parts,), jnp.float32, smallest / len(cuts), top_value / len(cuts))
        gain = gain * jnp.repeat(jnp.exp(heights), shape[axis_at] // parts).reshape((-1,) + (1,) * (len(shape) - 1 - axis_at))
    return gain


def noise(rng, extent, width, most, cuts=(), held_as=jnp.bfloat16):
    array = width * jax.random.normal(rng, extent, jnp.float32)
    if cuts:
        array = array * shard_levels(rng, extent, cuts, -0.22, 0.18)
    return jnp.clip(array, -most, most).astype(held_as)


def setup_inputs(seed: int = 0) -> dict:
    key_of = jax.random.split(jax.random.key(seed), 12)
    return {
        "gate_pre": noise(key_of[0], (TOKENS, FF), 1.0, 6.0, ((0, 32),)),
        "up_pre": noise(key_of[1], (TOKENS, FF), 1.0, 6.0, ((0, 32),)),
        "grad_out": noise(key_of[2], (TOKENS, D), 1.0, 6.0, ((0, 32),)),
        "token_ids": draw_token_ids(jax.random.fold_in(key_of[11], 71), 0),
        "step_count": jax.random.randint(key_of[4], (1,), 0, 1000).astype(jnp.int32),
        "island_drift": noise(key_of[5], (N_ISLAND, FF, D), 0.3, 4.0, ((0, 4), (1, 8)), jnp.float32),
        "adam_m": noise(key_of[6], (N_ISLAND, FF, D), ((FF * TOK_ISLAND) ** -0.5), 0.015625, ((0, 4), (1, 8)), jnp.float32),
        "adam_v": jnp.clip(jnp.exp(math.log(6.103515488575795e-07) - 2.7725887 * jax.random.uniform(key_of[7], (N_ISLAND, FF, D), jnp.float32) ** shard_levels(key_of[7], (N_ISLAND, FF, D), ((0, 4), (1, 8)), -0.2, 0.2)), 3.814697180359872e-08, 6.103515488575795e-07),
        "anchor": noise(key_of[8], (FF, D), 1.0, 6.0, ((0, 8),), jnp.float32),
        "momentum": noise(key_of[9], (FF, D), 0.3, 4.0, ((0, 8),), jnp.float32),
        "next_hidden": noise(key_of[10], (TOKENS, FF), 1.0, 6.0, ((0, 32),)),
    }


peak_rate = 0.25
beta_one = 0.9
beta_two = 0.95
adam_eps = 1e-08
decay_rate = 0.1
outer_rate = 0.7
outer_beta = 0.9

def reference(gate_pre, up_pre, grad_out, token_ids, step_count, island_drift, adam_m, adam_v, anchor, momentum, next_hidden):
    factor = float(FF) ** (-0.5)
    hidden = (jax.nn.silu(gate_pre.astype(jnp.float32)) * up_pre.astype(jnp.float32)).astype(jnp.bfloat16)
    live_rows = token_ids != 0
    masked = jnp.where(live_rows[:, None], grad_out, jnp.zeros_like(grad_out))
    moment = step_count[0].astype(jnp.float32)
    inner_rate = peak_rate * jnp.minimum(1.0, (moment + 1.0) / 100.0) * (0.1 + 0.45 * (1.0 + jnp.cos(math.pi * moment / 1000.0)))
    bias_one = 1.0 - jnp.power(jnp.float32(beta_one), moment + 1.0)
    bias_two = 1.0 - jnp.power(jnp.float32(beta_two), moment + 1.0)
    summed = jnp.zeros((FF, D), jnp.float32)
    shares = []
    for island in range(N_ISLAND):
        lower = island * TOK_ISLAND
        upper = lower + TOK_ISLAND
        tally = jnp.sum(live_rows[lower:upper].astype(jnp.float32))
        shares.append(tally / float(TOK_ISLAND))
        gradient = lax.dot_general(hidden[lower:upper], masked[lower:upper], (((0,), (0,)), ((), ())), preferred_element_type=jnp.float32) * factor / tally
        first_moment = beta_one * adam_m[island] + (1.0 - beta_one) * gradient
        second_moment = beta_two * adam_v[island] + (1.0 - beta_two) * gradient * gradient
        direction = first_moment / bias_one / (jnp.sqrt(second_moment / bias_two) + adam_eps)
        params = anchor + island_drift[island]
        updated = params - inner_rate * (direction + decay_rate * params)
        summed = summed + (anchor - updated)
    mean_change = summed / N_ISLAND
    new_momentum = outer_beta * momentum + mean_change
    new_anchor = anchor - outer_rate * (mean_change + outer_beta * new_momentum)
    weights = new_anchor.astype(jnp.bfloat16)
    next_out = (jnp.dot(next_hidden, weights, preferred_element_type=jnp.float32) * factor).astype(jnp.bfloat16)
    live_share = jnp.stack(shares).astype(jnp.float32)
    return (new_anchor, new_momentum, next_out, live_share)
```

```python
import functools
import math

import jax
import jax.numpy as jnp
from jax import lax
from jax.experimental import pallas as pl
from jax.experimental.pallas import tpu as pltpu
from jax.sharding import PartitionSpec as P

peak_rate = 0.25
beta_one = 0.9
beta_two = 0.95
adam_eps = 1e-08
decay_rate = 0.1
outer_rate = 0.7
outer_beta = 0.9

MESH = pl.DeviceIdType.MESH
CORES = 2


def exchange(
    n_shard, n_island, chunks, wide, factor, slot_total,
    scal, gate, up, tok, gout, drift, adam_m, adam_v, anchor, mom,
    w_out, na_out, nm_out, share_out,
    h_t, g_buf, d_buf, m_buf, v_buf, a_buf, o_buf,
    own, p_send, p_recv, recv,
    x_send, x_recv, w_buf, cnt, tal,
    g_sem, s_sem, o_sem, p_s, p_r, f_s, f_r,
    x_s, x_r, a_s, a_r, b_s, b_r, c_s, c_r, t_s, t_r, out_sem,
):
    chips = n_shard // CORES
    rows = anchor.shape[0]
    shard = lax.axis_index("shard")
    island = lax.axis_index("island")
    chip = shard // CORES
    core = shard % CORES
    span = chunks * wide

    def at(sh, isl):
        return {"shard": sh, "island": isl}

    def remote(src, dst, ss, rs, sh, isl):
        return pltpu.make_async_remote_copy(
            src_ref=src, dst_ref=dst, send_sem=ss, recv_sem=rs,
            device_id=at(sh, isl), device_id_type=MESH)

    def columns(c, i):
        return pl.ds(pl.multiple_of(i * span + c * wide, wide), wide)

    def load_g(c, i):
        return pltpu.make_async_copy(gout.at[:, columns(c, i)], g_buf.at[c, i], g_sem.at[c, i])

    def load_state(c, i):
        col = columns(c, i)
        return [
            pltpu.make_async_copy(src, dst.at[c, i], s_sem.at[j, c, i])
            for j, (src, dst) in enumerate((
                (drift.at[0, :, col], d_buf), (adam_m.at[0, :, col], m_buf),
                (adam_v.at[0, :, col], v_buf), (anchor.at[:, col], a_buf)))
        ]

    def load_mom(c):
        return pltpu.make_async_copy(mom.at[:, columns(c, island)], o_buf.at[c], o_sem.at[c])

    def each(total, body):
        lax.fori_loop(0, total, lambda j, _: (body(j), 0)[1], 0)

    each(chunks, lambda c: each(n_island, lambda i: load_g(c, i).start()))

    def start_state(c):
        each(n_island, lambda i: [cp.start() for cp in load_state(c, i)])
        load_mom(c).start()

    each(chunks, start_state)

    barrier = pltpu.get_barrier_semaphore()
    for off in range(1, n_shard):
        pl.semaphore_signal(barrier, inc=1, device_id=at((shard + off) % n_shard, island), device_id_type=MESH)
    for off in range(1, n_island):
        pl.semaphore_signal(barrier, inc=1, device_id=at(shard, (island + off) % n_island), device_id_type=MESH)

    pre = gate[...].astype(jnp.float32)
    hidden = (pre / (1.0 + jnp.exp(-pre))) * up[...].astype(jnp.float32)
    live = tok[...] != 0
    turned = jnp.where(live, hidden.T, 0.0).astype(jnp.bfloat16)
    for z in range(chips):
        for b in range(CORES):
            h_t[b, pl.ds(z * rows, rows), :] = turned[(z * CORES + b) * rows:(z * CORES + b + 1) * rows]
    cnt[...] = jnp.full(cnt.shape, jnp.sum(live.astype(jnp.float32)), jnp.float32)

    pl.semaphore_wait(barrier, n_shard - 1 + n_island - 1)

    def count_copy(off):
        return remote(cnt, tal.at[off], t_s.at[off], t_r.at[off], (shard + off) % n_shard, island)

    for off in range(1, n_shard):
        count_copy(off).start()

    partner = chip * CORES + (1 - core)

    def pair_copy(c):
        return remote(p_send.at[c], p_recv.at[c], p_s.at[c], p_r.at[c], partner, island)

    def right_copy(c, d):
        return remote(own.at[c, d], recv.at[c, d], f_s.at[c, d], f_r.at[c, d],
                      lax.rem(shard + CORES, n_shard), island)

    def left_copy(c, d):
        slot = jnp.where(d == chip - 1, chips, d)
        return remote(own.at[c, d], recv.at[c, slot], f_s.at[c, d], f_r.at[c, slot],
                      lax.rem(shard + n_shard - CORES, n_shard), island)

    def change_copy(c, off):
        j = (island + off) % n_island
        return remote(x_send.at[c, j], x_recv.at[c, off], x_s.at[c, off], x_r.at[c, off], shard, j)

    def line_copy(c, off):
        to = ((chip + off) % chips) * CORES + core
        mine = w_buf.at[c, island, chip, core]
        return remote(mine, mine, a_s.at[c, off], a_r.at[c, off], to, island)

    def island_copy(c, off):
        mine = w_buf.at[c, island, :, core]
        return remote(mine, mine, b_s.at[c, off], b_r.at[c, off], shard, (island + off) % n_island)

    def core_copy(c):
        mine = w_buf.at[c, :, :, core]
        return remote(mine, mine, c_s.at[c], c_r.at[c], partner, island)

    def store_copy(c):
        return pltpu.make_async_copy(w_buf.at[c], w_out.at[c], out_sem.at[c])

    def within(c, body):
        @pl.when((c >= 0) & (c < chunks))
        def _():
            body(c)

    def product(c):
        def piece(i):
            load_g(c, i).wait()
            g = g_buf[c, i]
            away = jnp.dot(h_t[1 - core], g, preferred_element_type=jnp.float32) * factor
            for d in range(chips):
                p_send[c, d, i] = away[d * rows:(d + 1) * rows]
            here = jnp.dot(h_t[core], g, preferred_element_type=jnp.float32) * factor
            for d in range(chips):
                own[c, d, i] = here[d * rows:(d + 1) * rows]

        each(n_island, piece)
        pair_copy(c).start()

    def add_pair(c):
        pair_copy(c).wait_recv()

        def piece(d):
            own[c, d] = own[c, d] + p_recv[c, d]

        each(chips, piece)

    def arrived(c, slot, d):
        remote(own.at[c, d], recv.at[c, slot], f_s.at[c, d], f_r.at[c, slot], partner, island).wait_recv()
        own[c, d] = own[c, d] + recv[c, slot]

    def flow(c, copy, order, first, ahead):
        for d in order:
            @pl.when(ahead(d))
            def _():
                @pl.when(jnp.logical_not(first))
                def _():
                    arrived(c, d, d)

                copy(c, d).start()

    def right(c):
        flow(c, right_copy, range(chips - 1, -1, -1), chip == 0, lambda d: d > chip)

    def left(c):
        flow(c, left_copy, range(chips), chip == chips - 1, lambda d: d < chip)

    def inner(c):
        @pl.when(chip > 0)
        def _():
            arrived(c, chip, chip)

        @pl.when(chip < chips - 1)
        def _():
            arrived(c, chips, chip)

        tally = cnt[0:1, 0:1]
        for off in range(1, n_shard):
            tally = tally + tal[off, 0:1, 0:1]
        rate, bias_one, bias_two = scal[0], scal[1], scal[2]

        def piece(i):
            for cp in load_state(c, i):
                cp.wait()
            gradient = own[c, chip, i] / tally
            first = beta_one * m_buf[c, i] + (1.0 - beta_one) * gradient
            second = beta_two * v_buf[c, i] + (1.0 - beta_two) * gradient * gradient
            direction = first / bias_one / (jnp.sqrt(second / bias_two) + adam_eps)
            held = a_buf[c, i]
            params = held + d_buf[c, i]
            updated = params - rate * (direction + decay_rate * params)
            x_send[c, i] = held - updated

        each(n_island, piece)
        for off in range(1, n_island):
            change_copy(c, off).start()

    def outer(c):
        total = x_send[c, island]
        for off in range(1, n_island):
            change_copy(c, off).wait_recv()
            total = total + x_recv[c, off]
        mean = total / n_island
        load_mom(c).wait()
        momentum = outer_beta * o_buf[c] + mean
        fresh = a_buf[c, island] - outer_rate * (mean + outer_beta * momentum)
        nm_out[c] = momentum
        na_out[c] = fresh
        w_buf[c, island, chip, core] = fresh.astype(jnp.bfloat16)
        for off in range(1, chips):
            line_copy(c, off).start()

    def spread(c):
        for off in range(1, chips):
            line_copy(c, off).wait_recv()
        for off in range(1, n_island):
            island_copy(c, off).start()

    def pair_up(c):
        for off in range(1, n_island):
            island_copy(c, off).wait_recv()
        core_copy(c).start()

    def finish(c):
        core_copy(c).wait_recv()
        store_copy(c).start()

    def step(t):
        within(t, product)
        within(t - 1, add_pair)
        within(t - 1 - chip, right)
        within(t - 1 - (chips - 1 - chip), left)

        @pl.when(t == chips)
        def _():
            for off in range(1, n_shard):
                count_copy(off).wait_recv()

        within(t - chips, inner)
        within(t - chips - 1, outer)
        within(t - chips - 2, spread)
        within(t - chips - 3, pair_up)
        within(t - chips - 4, finish)

    each(chunks + chips + 4, step)

    tally = cnt[...]
    for off in range(1, n_shard):
        tally = tally + tal[off]
    share_out[...] = tally / slot_total

    for off in range(1, n_shard):
        count_copy(off).wait_send()

    def drain(c):
        pair_copy(c).wait_send()
        for d in range(chips):
            @pl.when(d > chip)
            def _():
                right_copy(c, d).wait_send()

            @pl.when(d < chip)
            def _():
                left_copy(c, d).wait_send()
        for off in range(1, n_island):
            change_copy(c, off).wait_send()
            island_copy(c, off).wait_send()
        for off in range(1, chips):
            line_copy(c, off).wait_send()
        core_copy(c).wait_send()
        store_copy(c).wait()

    each(chunks, drain)


def forward(chunks, wide, factor, nh, w, na, nm, share, out, na_out, nm_out, share_out):
    @pl.when(pl.program_id(0) == 0)
    def _():
        for c in range(chunks):
            na_out[:, c * wide:(c + 1) * wide] = na[c]
            nm_out[:, c * wide:(c + 1) * wide] = nm[c]
        share_out[...] = share[...]

    pair = 2 if chunks % 2 == 0 else 1
    for c in range(0, chunks, pair):
        block = jnp.concatenate(
            [w[c + j, 0].reshape(nh.shape[1], wide) for j in range(pair)], axis=1)
        made = jnp.dot(nh[...], block, preferred_element_type=jnp.float32) * factor
        out[:, c * wide:(c + pair) * wide] = made.astype(jnp.bfloat16)


def shards(
    n_shard, n_island,
    gate_pre, up_pre, grad_out, token_ids, step_count, island_drift,
    adam_m, adam_v, anchor, momentum, next_hidden,
):
    rows, width = anchor.shape
    tokens, hidden_units = gate_pre.shape
    chips = n_shard // CORES
    span = width // n_island
    wide = min(128, span)
    chunks = span // wide
    factor = float(hidden_units) ** (-0.5)
    slot_total = float(tokens * n_shard)
    moment = step_count[0].astype(jnp.float32)
    rate = (
        peak_rate
        * jnp.minimum(1.0, (moment + 1.0) / 100.0)
        * (0.1 + 0.45 * (1.0 + jnp.cos(math.pi * moment / 1000.0)))
    )
    scal = jnp.stack([
        rate,
        1.0 - jnp.power(jnp.float32(beta_one), moment + 1.0),
        1.0 - jnp.power(jnp.float32(beta_two), moment + 1.0),
    ])
    f32, bf16 = jnp.float32, jnp.bfloat16
    any_space = pl.BlockSpec(memory_space=pl.ANY)
    vmem = pl.BlockSpec(memory_space=pltpu.VMEM)
    smem = pl.BlockSpec(memory_space=pltpu.SMEM)
    dma = pltpu.SemaphoreType.DMA
    state = pltpu.VMEM((chunks, n_island, rows, wide), f32)
    lines = pltpu.VMEM((chunks, chips, n_island, rows, wide), f32)
    w_shape = (chunks, n_island, chips, CORES, rows, wide)
    w, na, nm, share = pl.pallas_call(
        functools.partial(exchange, n_shard, n_island, chunks, wide, factor, slot_total),
        out_shape=(
            jax.ShapeDtypeStruct(w_shape, bf16),
            jax.ShapeDtypeStruct((chunks, rows, wide), f32),
            jax.ShapeDtypeStruct((chunks, rows, wide), f32),
            jax.ShapeDtypeStruct((8, 128), f32),
        ),
        in_specs=[smem, vmem, vmem, vmem] + [any_space] * 6,
        out_specs=(any_space, vmem, vmem, vmem),
        scratch_shapes=[
            pltpu.VMEM((CORES, chips * rows, tokens), bf16),
            pltpu.VMEM((chunks, n_island, tokens, wide), bf16),
            state, state, state, state,
            pltpu.VMEM((chunks, rows, wide), f32),
            lines, lines, lines,
            pltpu.VMEM((chunks, chips + 1, n_island, rows, wide), f32),
            state,
            pltpu.VMEM((chunks, n_island, rows, wide), f32),
            pltpu.VMEM(w_shape, bf16),
            pltpu.VMEM((8, 128), f32),
            pltpu.VMEM((n_shard, 8, 128), f32),
            dma((chunks, n_island)), dma((4, chunks, n_island)), dma((chunks,)),
            dma((chunks,)), dma((chunks,)),
            dma((chunks, chips)), dma((chunks, chips + 1)),
            dma((chunks, n_island)), dma((chunks, n_island)),
            dma((chunks, chips)), dma((chunks, chips)),
            dma((chunks, n_island)), dma((chunks, n_island)),
            dma((chunks,)), dma((chunks,)),
            dma((n_shard,)), dma((n_shard,)),
            dma((chunks,)),
        ],
        compiler_params=pltpu.CompilerParams(
            collective_id=0, has_side_effects=True, vmem_limit_bytes=62 * 1024 * 1024),
    )(scal, gate_pre, up_pre, token_ids.reshape(1, tokens), grad_out,
      island_drift, adam_m, adam_v, anchor, momentum)

    def whole(shape):
        return pl.BlockSpec(shape, lambda i: (0,) * len(shape))

    next_out, new_anchor, new_momentum, share = pl.pallas_call(
        functools.partial(forward, chunks, wide, factor),
        grid=(n_island,),
        out_shape=(
            jax.ShapeDtypeStruct((next_hidden.shape[0], width), bf16),
            jax.ShapeDtypeStruct((rows, span), f32),
            jax.ShapeDtypeStruct((rows, span), f32),
            jax.ShapeDtypeStruct((8, 128), f32),
        ),
        in_specs=[
            whole(next_hidden.shape),
            pl.BlockSpec((chunks, 1, chips, CORES, rows, wide), lambda i: (0, i, 0, 0, 0, 0)),
            whole(na.shape), whole(nm.shape), whole(share.shape),
        ],
        out_specs=(
            pl.BlockSpec((next_hidden.shape[0], span), lambda i: (0, i)),
            whole((rows, span)), whole((rows, span)), whole((8, 128)),
        ),
    )(next_hidden, w, na, nm, share)
    return new_anchor, new_momentum, next_out, share[0, 0:1]


def solution(mesh):
    in_specs = (
        P(("island", "shard"), None),
        P(("island", "shard"), None),
        P(("island", "shard"), None),
        P(("island", "shard")),
        P(),
        P("island", "shard", None),
        P("island", "shard", None),
        P("island", "shard", None),
        P("shard", None),
        P("shard", None),
        P(("island", "shard"), None),
    )
    out_specs = (
        P("shard", "island"),
        P("shard", "island"),
        P(("island", "shard"), None),
        P("island"),
    )
    body = functools.partial(shards, mesh.shape["shard"], mesh.shape["island"])
    return jax.shard_map(body, mesh=mesh, in_specs=in_specs, out_specs=out_specs, check_vma=False)
```

```python
import functools
import math

import jax
import jax.numpy as jnp
from jax import lax
from jax.experimental import pallas as pl
from jax.experimental.pallas import tpu as pltpu
from jax.sharding import PartitionSpec as P

peak_rate = 0.25
beta_one = 0.9
beta_two = 0.95
adam_eps = 1e-08
decay_rate = 0.1
outer_rate = 0.7
outer_beta = 0.9

MESH = pl.DeviceIdType.MESH
CORES = 2


def exchange(
    n_shard, n_island, chunks, wide, factor, slot_total,
    scal, gate, up, tok, gout, drift, adam_m, adam_v, anchor, mom,
    w_out, na_out, nm_out, share_out,
    h_t, g_buf, d_buf, m_buf, v_buf, a_buf, o_buf,
    own, p_send, p_recv, recv,
    x_send, x_recv, w_buf, cnt, tal,
    g_sem, s_sem, p_s, p_r, f_s, f_r,
    x_s, x_r, a_s, a_r, b_s, b_r, c_s, c_r, t_s, t_r, out_sem,
):
    chips = n_shard // CORES
    rows = anchor.shape[0]
    shard = lax.axis_index("shard")
    island = lax.axis_index("island")
    chip = shard // CORES
    core = shard % CORES
    span = chunks * wide

    def at(sh, isl):
        return {"shard": sh, "island": isl}

    def remote(src, dst, ss, rs, sh, isl):
        return pltpu.make_async_remote_copy(
            src_ref=src, dst_ref=dst, send_sem=ss, recv_sem=rs,
            device_id=at(sh, isl), device_id_type=MESH)

    def columns(c, i):
        return pl.ds(pl.multiple_of(i * span + c * wide, wide), wide)

    def load_g(c, i):
        return pltpu.make_async_copy(gout.at[:, columns(c, i)], g_buf.at[c, i], g_sem.at[c, i])

    loads = [
        pltpu.make_async_copy(src, dst, s_sem.at[j])
        for j, (src, dst) in enumerate((
            (drift.at[0], d_buf), (adam_m.at[0], m_buf), (adam_v.at[0], v_buf), (anchor, a_buf),
            (mom.at[:, pl.ds(pl.multiple_of(island * span, span), span)], o_buf)))
    ]

    def each(total, body):
        lax.fori_loop(0, total, lambda j, _: (body(j), 0)[1], 0)

    def start_g(c):
        for i in range(n_island):
            load_g(c, i).start()

    ahead = min(4, chunks)
    each(ahead, start_g)

    barrier = pltpu.get_barrier_semaphore()
    for off in range(1, n_shard):
        pl.semaphore_signal(barrier, inc=1, device_id=at((shard + off) % n_shard, island), device_id_type=MESH)
    for off in range(1, n_island):
        pl.semaphore_signal(barrier, inc=1, device_id=at(shard, (island + off) % n_island), device_id_type=MESH)

    pre = gate[...].astype(jnp.float32)
    hidden = (pre / (1.0 + jnp.exp(-pre))) * up[...].astype(jnp.float32)
    live = tok[...] != 0
    turned = jnp.where(live, hidden.T, 0.0).astype(jnp.bfloat16)
    for z in range(chips):
        for b in range(CORES):
            h_t[b, pl.ds(z * rows, rows), :] = turned[(z * CORES + b) * rows:(z * CORES + b + 1) * rows]
    for cp in loads:
        cp.start()
    cnt[...] = jnp.full(cnt.shape, jnp.sum(live.astype(jnp.float32)), jnp.float32)

    pl.semaphore_wait(barrier, n_shard - 1 + n_island - 1)

    def count_copy(off):
        return remote(cnt, tal.at[off], t_s.at[off], t_r.at[off], (shard + off) % n_shard, island)

    for off in range(1, n_shard):
        count_copy(off).start()

    partner = chip * CORES + (1 - core)

    def pair_copy(c):
        return remote(p_send.at[c], p_recv.at[c], p_s.at[c], p_r.at[c], partner, island)

    def right_copy(c, d):
        return remote(own.at[c, d], recv.at[c, d], f_s.at[c, d], f_r.at[c, d],
                      lax.rem(shard + CORES, n_shard), island)

    def left_copy(c, d):
        slot = jnp.where(d == chip - 1, chips, d)
        return remote(own.at[c, d], recv.at[c, slot], f_s.at[c, d], f_r.at[c, slot],
                      lax.rem(shard + n_shard - CORES, n_shard), island)

    def change_copy(c, off):
        j = (island + off) % n_island
        return remote(x_send.at[c, j], x_recv.at[c, off], x_s.at[c, off], x_r.at[c, off], shard, j)

    def line_copy(c, off):
        to = ((chip + off) % chips) * CORES + core
        mine = w_buf.at[c, island, chip, core]
        return remote(mine, mine, a_s.at[c, off], a_r.at[c, off], to, island)

    def island_copy(c, off):
        mine = w_buf.at[c, island, :, core]
        return remote(mine, mine, b_s.at[c, off], b_r.at[c, off], shard, (island + off) % n_island)

    def core_copy(c):
        mine = w_buf.at[c, :, :, core]
        return remote(mine, mine, c_s.at[c], c_r.at[c], partner, island)

    def store_copy(c):
        return pltpu.make_async_copy(w_buf.at[c], w_out.at[c], out_sem.at[c])

    def within(c, body):
        @pl.when((c >= 0) & (c < chunks))
        def _():
            body(c)

    def product(c):
        def piece(i):
            load_g(c, i).wait()
            g = g_buf[c, i]
            away = jnp.dot(h_t[1 - core], g, preferred_element_type=jnp.float32) * factor
            for d in range(chips):
                p_send[c, d, i] = away[d * rows:(d + 1) * rows]
            here = jnp.dot(h_t[core], g, preferred_element_type=jnp.float32) * factor
            for d in range(chips):
                own[c, d, i] = here[d * rows:(d + 1) * rows]

        each(n_island, piece)
        pair_copy(c).start()

    def add_pair(c):
        pair_copy(c).wait_recv()

        def piece(d):
            own[c, d] = own[c, d] + p_recv[c, d]

        each(chips, piece)

    def arrived(c, slot, d):
        remote(own.at[c, d], recv.at[c, slot], f_s.at[c, d], f_r.at[c, slot], partner, island).wait_recv()
        own[c, d] = own[c, d] + recv[c, slot]

    def flow(c, copy, order, first, ahead):
        for d in order:
            @pl.when(ahead(d))
            def _():
                @pl.when(jnp.logical_not(first))
                def _():
                    arrived(c, d, d)

                copy(c, d).start()

    def right(c):
        flow(c, right_copy, range(chips - 1, -1, -1), chip == 0, lambda d: d > chip)

    def left(c):
        flow(c, left_copy, range(chips), chip == chips - 1, lambda d: d < chip)

    def inner(c):
        @pl.when(chip > 0)
        def _():
            arrived(c, chip, chip)

        @pl.when(chip < chips - 1)
        def _():
            arrived(c, chips, chip)

        tally = cnt[0:1, 0:1]
        for off in range(1, n_shard):
            tally = tally + tal[off, 0:1, 0:1]
        rate, bias_one, bias_two = scal[0], scal[1], scal[2]

        def piece(i):
            col = columns(c, i)
            gradient = own[c, chip, i] / tally
            first = beta_one * m_buf[:, col] + (1.0 - beta_one) * gradient
            second = beta_two * v_buf[:, col] + (1.0 - beta_two) * gradient * gradient
            direction = first / bias_one / (jnp.sqrt(second / bias_two) + adam_eps)
            held = a_buf[:, col]
            params = held + d_buf[:, col]
            updated = params - rate * (direction + decay_rate * params)
            x_send[c, i] = held - updated

        each(n_island, piece)
        for off in range(1, n_island):
            change_copy(c, off).start()

    def outer(c):
        total = x_send[c, island]
        for off in range(1, n_island):
            change_copy(c, off).wait_recv()
            total = total + x_recv[c, off]
        mean = total / n_island
        piece = pl.ds(pl.multiple_of(c * wide, wide), wide)
        momentum = outer_beta * o_buf[:, piece] + mean
        fresh = a_buf[:, columns(c, island)] - outer_rate * (mean + outer_beta * momentum)
        nm_out[c] = momentum
        na_out[c] = fresh
        w_buf[c, island, chip, core] = fresh.astype(jnp.bfloat16)
        for off in range(1, chips):
            line_copy(c, off).start()

    def spread(c):
        for off in range(1, chips):
            line_copy(c, off).wait_recv()
        for off in range(1, n_island):
            island_copy(c, off).start()

    def pair_up(c):
        for off in range(1, n_island):
            island_copy(c, off).wait_recv()
        core_copy(c).start()

    def finish(c):
        core_copy(c).wait_recv()
        store_copy(c).start()

    def drain(c):
        pair_copy(c).wait_send()
        for d in range(chips):
            @pl.when(d > chip)
            def _():
                right_copy(c, d).wait_send()

            @pl.when(d < chip)
            def _():
                left_copy(c, d).wait_send()
        for off in range(1, n_island):
            change_copy(c, off).wait_send()
            island_copy(c, off).wait_send()
        for off in range(1, chips):
            line_copy(c, off).wait_send()
        core_copy(c).wait_send()
        store_copy(c).wait()

    late = 2

    def step(t):
        within(t, product)
        @pl.when(t + ahead < chunks)
        def _():
            start_g(t + ahead)

        within(t - 1, add_pair)
        within(t - 1 - chip, right)
        within(t - 1 - (chips - 1 - chip), left)

        @pl.when(t == chips)
        def _():
            for off in range(1, n_shard):
                count_copy(off).wait_recv()
            for cp in loads:
                cp.wait()

        within(t - chips, inner)
        within(t - chips - 1, outer)
        within(t - chips - 2, spread)
        within(t - chips - 3, pair_up)
        within(t - chips - 4, finish)
        within(t - chips - 4 - late, drain)

    each(chunks + chips + 4, step)

    tally = cnt[...]
    for off in range(1, n_shard):
        tally = tally + tal[off]
    share_out[...] = tally / slot_total

    for off in range(1, n_shard):
        count_copy(off).wait_send()

    each(min(late, chunks), lambda j: drain(chunks - min(late, chunks) + j))


def forward(chunks, parts, wide, factor, nh, w, na, nm, share, out, na_out, nm_out, share_out):
    @pl.when((pl.program_id(0) == 0) & (pl.program_id(1) == 0))
    def _():
        for c in range(chunks):
            na_out[:, c * wide:(c + 1) * wide] = na[c]
            nm_out[:, c * wide:(c + 1) * wide] = nm[c]
        share_out[0] = share[0, 0]

    count = chunks // parts
    pair = 2 if count % 2 == 0 else 1
    for c in range(0, count, pair):
        block = jnp.concatenate(
            [w[c + j, 0].reshape(nh.shape[1], wide) for j in range(pair)], axis=1)
        made = jnp.dot(nh[...], block, preferred_element_type=jnp.float32) * factor
        out[:, c * wide:(c + pair) * wide] = made.astype(jnp.bfloat16)


def shards(
    n_shard, n_island,
    gate_pre, up_pre, grad_out, token_ids, step_count, island_drift,
    adam_m, adam_v, anchor, momentum, next_hidden,
):
    rows, width = anchor.shape
    tokens, hidden_units = gate_pre.shape
    chips = n_shard // CORES
    span = width // n_island
    wide = min(128, span)
    chunks = span // wide
    factor = float(hidden_units) ** (-0.5)
    slot_total = float(tokens * n_shard)
    moment = step_count[0].astype(jnp.float32)
    rate = (
        peak_rate
        * jnp.minimum(1.0, (moment + 1.0) / 100.0)
        * (0.1 + 0.45 * (1.0 + jnp.cos(math.pi * moment / 1000.0)))
    )
    scal = jnp.stack([
        rate,
        1.0 - jnp.power(jnp.float32(beta_one), moment + 1.0),
        1.0 - jnp.power(jnp.float32(beta_two), moment + 1.0),
    ])
    f32, bf16 = jnp.float32, jnp.bfloat16
    any_space = pl.BlockSpec(memory_space=pl.ANY)
    vmem = pl.BlockSpec(memory_space=pltpu.VMEM)
    smem = pl.BlockSpec(memory_space=pltpu.SMEM)
    dma = pltpu.SemaphoreType.DMA
    held = pltpu.VMEM((rows, width), f32)
    state = pltpu.VMEM((chunks, n_island, rows, wide), f32)
    lines = pltpu.VMEM((chunks, chips, n_island, rows, wide), f32)
    w_shape = (chunks, n_island, chips, CORES, rows, wide)
    w, na, nm, share = pl.pallas_call(
        functools.partial(exchange, n_shard, n_island, chunks, wide, factor, slot_total),
        out_shape=(
            jax.ShapeDtypeStruct(w_shape, bf16),
            jax.ShapeDtypeStruct((chunks, rows, wide), f32),
            jax.ShapeDtypeStruct((chunks, rows, wide), f32),
            jax.ShapeDtypeStruct((8, 128), f32),
        ),
        in_specs=[smem, vmem, vmem, vmem] + [any_space] * 6,
        out_specs=(any_space, vmem, vmem, vmem),
        scratch_shapes=[
            pltpu.VMEM((CORES, chips * rows, tokens), bf16),
            pltpu.VMEM((chunks, n_island, tokens, wide), bf16),
            held, held, held, held,
            pltpu.VMEM((rows, span), f32),
            lines, lines, lines,
            pltpu.VMEM((chunks, chips + 1, n_island, rows, wide), f32),
            state,
            pltpu.VMEM((chunks, n_island, rows, wide), f32),
            pltpu.VMEM(w_shape, bf16),
            pltpu.VMEM((8, 128), f32),
            pltpu.VMEM((n_shard, 8, 128), f32),
            dma((chunks, n_island)), dma((5,)),
            dma((chunks,)), dma((chunks,)),
            dma((chunks, chips)), dma((chunks, chips + 1)),
            dma((chunks, n_island)), dma((chunks, n_island)),
            dma((chunks, chips)), dma((chunks, chips)),
            dma((chunks, n_island)), dma((chunks, n_island)),
            dma((chunks,)), dma((chunks,)),
            dma((n_shard,)), dma((n_shard,)),
            dma((chunks,)),
        ],
        compiler_params=pltpu.CompilerParams(
            collective_id=0, has_side_effects=True, vmem_limit_bytes=62 * 1024 * 1024),
    )(scal, gate_pre, up_pre, token_ids.reshape(1, tokens), grad_out,
      island_drift, adam_m, adam_v, anchor, momentum)

    def whole(shape):
        return pl.BlockSpec(shape, lambda i, h: (0,) * len(shape))

    parts = 2 if chunks % 2 == 0 else 1
    count = chunks // parts
    next_out, new_anchor, new_momentum, live_share = pl.pallas_call(
        functools.partial(forward, chunks, parts, wide, factor),
        grid=(n_island, parts),
        out_shape=(
            jax.ShapeDtypeStruct((next_hidden.shape[0], width), bf16),
            jax.ShapeDtypeStruct((rows, span), f32),
            jax.ShapeDtypeStruct((rows, span), f32),
            jax.ShapeDtypeStruct((1,), f32),
        ),
        in_specs=[
            whole(next_hidden.shape),
            pl.BlockSpec((count, 1, chips, CORES, rows, wide), lambda i, h: (h, i, 0, 0, 0, 0)),
            whole(na.shape), whole(nm.shape), smem,
        ],
        out_specs=(
            pl.BlockSpec((next_hidden.shape[0], count * wide), lambda i, h: (0, i * parts + h)),
            whole((rows, span)), whole((rows, span)), smem,
        ),
    )(next_hidden, w, na, nm, share)
    return new_anchor, new_momentum, next_out, live_share


def solution(mesh):
    in_specs = (
        P(("island", "shard"), None),
        P(("island", "shard"), None),
        P(("island", "shard"), None),
        P(("island", "shard")),
        P(),
        P("island", "shard", None),
        P("island", "shard", None),
        P("island", "shard", None),
        P("shard", None),
        P("shard", None),
        P(("island", "shard"), None),
    )
    out_specs = (
        P("shard", "island"),
        P("shard", "island"),
        P(("island", "shard"), None),
        P("island"),
    )
    body = functools.partial(shards, mesh.shape["shard"], mesh.shape["island"])
    return jax.shard_map(body, mesh=mesh, in_specs=in_specs, out_specs=out_specs, check_vma=False)
```
